32 devices in a mesh: fsdp: 16 (over z, x, core), rep: 2 (over y).
Axes of the slice: x: 2, y: 2, z: 4, core: 2. Of those that a mesh axis runs over, the one named last changes fastest.
Arguments:
- layer_input: bfloat16 [128, 256, 768], P(('fsdp', 'rep')), may hold values from -6 to 6
- slot_valid: int32 [128, 256], P(('fsdp', 'rep')), may hold values from 0 to 1, as said below
- projections: bfloat16 [3, 768, 768], P(None, 'fsdp'), may hold values from -0.21875 to 0.21875
- out_weight: bfloat16 [768, 768], P('fsdp'), may hold values from -1.25 to 1.25
- vectors: bfloat16 [8, 768], P(None, 'fsdp'), may hold values from -2 to 2
- up_weight: bfloat16 [768, 3072], P('fsdp'), may hold values from -0.21875 to 0.21875
- up_bias: bfloat16 [3072], P('fsdp'), may hold values from -3 to 3
- down_weight: bfloat16 [3072, 768], P('fsdp'), may hold values from -0.109375 to 0.109375
- cotangent: bfloat16 [128, 256, 768], P(('fsdp', 'rep')), may hold values from -6 to 6
Outputs:
- output: bfloat16 [128, 256, 768], P(('fsdp', 'rep'))
- grad_input: bfloat16 [128, 256, 768], P(('fsdp', 'rep'))
- grad_projections: float32 [3, 768, 768], P(None, 'fsdp')
- grad_out_weight: float32 [768, 768], P('fsdp')
- grad_vectors: float32 [8, 768], P(None, 'fsdp')
- grad_up_weight: float32 [768, 3072], P('fsdp')
- grad_up_bias: float32 [3072], P('fsdp')
- grad_down_weight: float32 [3072, 768], P('fsdp')
The draws below stay inside these ranges and needn't reach their ends.
Inputs may be any that keep to these rules, and one draw needn't show every extreme that they name: `slot_valid`: in each sequence the first 128 slots are 1; of the next 128 slots the first k are 1 and the rest 0, with k from 10 to 100, both of which occur in every draw.
All inputs are finite; a program needn't handle non-finite values.
Results may differ from the reference program's by a relative error of at most 0.02.
Values may be sent and summed in bfloat16 or wider, within the bound.
No kernel may reach another device: no remote copies, remote signals or barrier semaphores. Data moves between devices by JAX's collectives and lax.ppermute only.
A program may use at most 192 MiB of HBM per device.

```python
import math
import jax
import jax.numpy as jnp
from jax import lax

D = 768
HEADS = 12
HD = 64
FF = 3072
TEXT = 128
REG_MIN = 10
REG_MAX = 100
SLOTS = 256
SEQS = 128


def draw_slot_valid(key, part):
    counts = jax.random.randint(key, (SEQS,), REG_MIN, REG_MAX + 1)
    counts = counts.at[0].set(REG_MAX).at[1].set(REG_MIN)
    slot_index = jnp.arange(SLOTS, dtype=jnp.int32)[None, :]
    region_live = (slot_index < TEXT) | (slot_index - TEXT < counts[:, None])
    return region_live.astype(jnp.int32)


def draw_vectors(key, part):
    noise = jnp.clip(jax.random.normal(key, (8, D), jnp.float32), -4.0, 4.0)
    is_gain = jnp.array([0.0, 0.0, 0.0, 1.0, 0.0, 0.0, 1.0, 0.0], jnp.float32)[:, None]
    return (noise * (0.5 - 0.4 * is_gain) + is_gain).astype(jnp.bfloat16)


def raised(result, stream_key, source, target, shards_of, factor):
    def block_of(axis_at):
        return (jnp.arange(result.shape[axis_at]) // (result.shape[axis_at] // shards_of)).reshape((-1,) + (1,) * (result.ndim - 1 - axis_at))

    first = jax.random.permutation(stream_key, shards_of)[block_of(target)]
    second = (block_of(target) + shards_of // 2) % shards_of
    return jnp.where((block_of(source) == first) | (block_of(source) == second), factor * result, result)


def steps_of(own_key, extent, split, low, high):
    level = 1.0
    for dim, parts in split:
        heights = jax.random.uniform(jax.random.fold_in(jax.random.fold_in(own_key, 6), dim), (parts,), jnp.float32, low / len(split), high / len(split))
        level = level * jnp.repeat(jnp.exp(heights), extent[dim] // parts).reshape((-1,) + (1,) * (len(extent) - 1 - dim))
    return level


def centred(key, dims, scale, most, split=(), kind=jnp.bfloat16):
    values = jax.random.normal(key, dims, jnp.float32) * scale
    if len(split) > 0:
        values = steps_of(key, dims, split, -0.22, 0.18) * values
    return jnp.clip(values, min=-most, max=most).astype(kind)


def heavy_noise(key, extent, scale, bound, split, heavy, kind=jnp.bfloat16):
    drawn = scale * jax.random.normal(key, extent, jnp.float32)
    if split:
        drawn = drawn * steps_of(key, extent, split, -0.22, 0.18)
    return jnp.clip(raised(drawn, jax.random.fold_in(key, 3), *heavy), -bound, bound).astype(kind)


def setup_inputs(seed: int = 0) -> dict:
    key_list = jax.random.split(jax.random.key(seed), 10)
    return {
        "layer_input": centred(key_list[0], (SEQS, SLOTS, D), 1.0, 6.0, ((0, 32),)),
        "slot_valid": draw_slot_valid(jax.random.fold_in(key_list[9], 71), 0),
        "projections": centred(key_list[2], (3, D, D), D ** -0.5, 0.21875, ((1, 16),)),
        "out_weight": centred(key_list[3], (D, D), (D // 32) ** -0.5, 1.25, ((0, 16),)),
        "vectors": draw_vectors(jax.random.fold_in(key_list[9], 71), 0),
        "up_weight": centred(key_list[5], (D, FF), D ** -0.5, 0.21875, ((0, 16),)),
        "up_bias": centred(key_list[6], (FF,), 0.5, 3.0, ((0, 16),)),
        "down_weight": centred(key_list[7], (FF, D), FF ** -0.5, 0.109375, ((0, 16),)),
        "cotangent": heavy_noise(key_list[8], (SEQS, SLOTS, D), 1.0, 6.0, ((0, 32),), (0, 2, 32, 2.75)),
    }


@jax.custom_vjp
def low(v):
    return lax.optimization_barrier(v.astype(jnp.bfloat16)).astype(jnp.float32)

@jax.custom_vjp
def low_back(v):
    return v

def low_keep(v):
    return (low(v), None)

def low_pass(kept, grad):
    return (grad,)

def back_keep(v):
    return (v, None)

def back_low(kept, grad):
    return (low(grad),)
low.defvjp(low_keep, low_pass)
low_back.defvjp(back_keep, back_low)
EPSILON = 1e-12
MASKED = -1e+30
HIGHEST = lax.Precision.HIGHEST

def normalize(values, gain, shift):
    centered = values - lax.optimization_barrier(jnp.mean(values, axis=-1, keepdims=True))
    spread = lax.optimization_barrier(jnp.mean(centered * centered, axis=-1, keepdims=True))
    return centered * lax.rsqrt(spread + EPSILON) * gain + shift

def project(values, weight):
    return jnp.einsum('gsd,de->gse', values, weight, precision=HIGHEST)

def layer_forward(seq_input, slot_valid, projections, out_weight, vectors, up_weight, up_bias, down_weight):
    bias_q, bias_v, bias_out, gain_one, shift_one, bias_down, gain_two, shift_two = vectors
    seq_count = seq_input.shape[0]
    score_scale = HD ** (-0.5)
    shape_heads = (seq_count, SLOTS, HEADS, HD)
    query_low = low(low_back(project(seq_input, projections[0]) + bias_q))
    key_low = low(low_back(project(seq_input, projections[1])))
    value_low = low(low_back(project(seq_input, projections[2]) + bias_v))
    scores = jnp.einsum('gqhe,gkhe->ghqk', query_low.reshape(shape_heads), key_low.reshape(shape_heads), precision=HIGHEST)
    scores = low_back(scores * score_scale)
    key_live = (slot_valid > 0)[:, None, None, :]
    scores = jnp.where(key_live, scores, MASKED)
    row_max = lax.optimization_barrier(jnp.max(scores, axis=-1, keepdims=True))
    exp_scores = jnp.exp(scores - row_max)
    probs_low = low(exp_scores / lax.optimization_barrier(jnp.sum(exp_scores, axis=-1, keepdims=True)))
    context = jnp.einsum('ghqk,gkhe->gqhe', probs_low, value_low.reshape(shape_heads), precision=HIGHEST)
    context = low(low_back(context.reshape(seq_count, SLOTS, D)))
    first_sum = low_back(seq_input + project(context, out_weight) + bias_out)
    normed = normalize(first_sum, gain_one, shift_one)
    hidden_pre = low_back(project(low(normed), up_weight) + up_bias)
    active_low = low(jax.nn.gelu(hidden_pre, approximate=False))
    second_sum = low_back(normed + project(active_low, down_weight) + bias_down)
    return normalize(second_sum, gain_two, shift_two) * slot_valid[:, :, None].astype(jnp.float32)

def reference(layer_input, slot_valid, projections, out_weight, vectors, up_weight, up_bias, down_weight, cotangent):
    seq_group = math.gcd(SEQS, 16)
    step_count = SEQS // seq_group
    params = tuple((weight_item.astype(jnp.float32) for weight_item in (projections, out_weight, vectors, up_weight, up_bias, down_weight)))
    seq_input = layer_input.astype(jnp.float32).reshape(step_count, seq_group, SLOTS, D)
    valid_groups = slot_valid.reshape(step_count, seq_group, SLOTS)
    grad_groups = cotangent.astype(jnp.float32).reshape(step_count, seq_group, SLOTS, D)

    def one_group(totals, item):
        group_input, group_valid, group_grad = item

        def forward(values, *weights):
            return layer_forward(values, group_valid, *weights)
        layer_out, pull_back = jax.vjp(forward, group_input, *params)
        grad_list = pull_back(group_grad)
        totals = tuple((total + grad_item for total, grad_item in zip(totals, grad_list[1:])))
        return (totals, (layer_out.astype(jnp.bfloat16), grad_list[0].astype(jnp.bfloat16)))
    zero_totals = tuple((jnp.zeros(weight_item.shape, jnp.float32) for weight_item in params))
    totals, (outputs, grad_inputs) = lax.scan(one_group, zero_totals, (seq_input, valid_groups, grad_groups))
    return (outputs.reshape(SEQS, SLOTS, D), grad_inputs.reshape(SEQS, SLOTS, D), totals[0], totals[1], totals[2], totals[3], totals[4], totals[5])
```

```python
from functools import partial

import jax
import jax.numpy as jnp
from jax import lax
from jax.experimental import pallas as pl
from jax.experimental.pallas import tpu as pltpu
from jax.sharding import PartitionSpec as P

HEADS = 12
HD = 64
PAIR = 2 * HD
SMALL_ROWS = 8
EPSILON = 1e-12
MASKED = -1e30
F32 = jnp.float32
BF16 = jnp.bfloat16
NN = (((1,), (0,)), ((), ()))
NT = (((1,), (1,)), ((), ()))
TN = (((0,), (0,)), ((), ()))


def mm(lhs, rhs, dims=NN):
    return lax.dot_general(lhs, rhs, dims, preferred_element_type=F32)


def square(ref, start, count):
    taken = ref[:, start : start + count, :]
    return taken.reshape(-1, taken.shape[-1])


def lane_masks(scale):
    lane = lax.broadcasted_iota(jnp.int32, (1, PAIR), 1)
    even = jnp.where(lane < HD, scale, 0.0).astype(BF16)
    odd = jnp.where(lane < HD, 0.0, scale).astype(BF16)
    return even, odd


def split_heads(pair, scale):
    even, odd = lane_masks(scale)
    return jnp.concatenate([pair * even, pair * odd], axis=0)


def join_heads(stacked):
    half = stacked.shape[0] // 2
    lane = lax.broadcasted_iota(jnp.int32, (half, PAIR), 1)
    return jnp.where(lane < HD, stacked[:half], stacked[half:])


def column_sum(values):
    return jnp.sum(values.astype(F32), axis=0, keepdims=True)


def attend_kernel(rows, x_ref, live_ref, w_ref, vec_ref, q_ref, k_ref, v_ref, p_ref, c_ref, f_ref):
    x = x_ref[0]
    q_ref[0] = (mm(x, square(w_ref, 0, rows)) + vec_ref[0:1]).astype(BF16)
    k_ref[0] = mm(x, square(w_ref, rows, rows)).astype(BF16)
    v_ref[0] = (mm(x, square(w_ref, 2 * rows, rows)) + vec_ref[1:2]).astype(BF16)
    live = live_ref[0] > 0.0
    for pair in range(HEADS // 2):
        cols = slice(pair * PAIR, (pair + 1) * PAIR)
        stacked = split_heads(q_ref[0, :, cols], HD**-0.5)
        scores = jnp.where(live, mm(k_ref[0, :, cols], stacked, NT), MASKED)
        raised = jnp.exp(scores - jnp.max(scores, axis=0, keepdims=True))
        weights = raised * (1.0 / jnp.sum(raised, axis=0, keepdims=True))
        p_ref[0, pair] = weights
        context = mm(weights.astype(BF16), v_ref[0, :, cols], TN)
        c_ref[0, :, cols] = join_heads(context).astype(BF16)
    f_ref[0] = x.astype(F32) + mm(c_ref[0], square(w_ref, 3 * rows, rows)) + vec_ref[2:3]


def centre(values):
    centered = values - jnp.mean(values, axis=-1, keepdims=True)
    spread = jnp.mean(centered * centered, axis=-1, keepdims=True)
    rate = lax.rsqrt(spread + EPSILON)
    return centered * rate, rate


def centre_back(grad, unit, rate):
    return rate * (
        grad
        - jnp.mean(grad, axis=-1, keepdims=True)
        - unit * jnp.mean(grad * unit, axis=-1, keepdims=True)
    )


def accumulate(ref, first, value):
    @pl.when(first)
    def _():
        ref[...] = value

    @pl.when(jnp.logical_not(first))
    def _():
        ref[...] += value


def feed_kernel(
    rows,
    hidden,
    f_ref,
    live_ref,
    cot_ref,
    w_ref,
    vec_ref,
    bias_ref,
    o_ref,
    act_ref,
    gh_ref,
    gs_ref,
    gf_ref,
    n_ref,
    small_ref,
    gbias_ref,
    slope_ref,
):
    width = f_ref.shape[-1]
    folds = act_ref.shape[-1] // width
    shards = max(width // hidden, 1)

    def up(fold):
        return square(w_ref, fold * rows, rows)

    def down(fold):
        base = folds * rows
        if hidden >= width:
            return square(w_ref, base + fold * width, width)
        taken = w_ref[fold * shards : (fold + 1) * shards, base : base + hidden, :]
        return taken.reshape(width, width)

    gain_one, shift_one, gain_two, shift_two = (vec_ref[i : i + 1] for i in (3, 4, 6, 7))
    unit_one, rate_one = centre(f_ref[...])
    normed = unit_one * gain_one + shift_one
    n_ref[...] = normed.astype(BF16)
    second = normed + vec_ref[5:6]
    for fold in range(folds):
        cols = slice(fold * width, (fold + 1) * width)
        pre = mm(n_ref[...], up(fold)) + bias_ref[:, cols]
        phi = 0.5 + 0.5 * lax.erf(pre * 0.7071067811865476)
        act = (pre * phi).astype(BF16)
        act_ref[:, cols] = act
        slope_ref[:, cols] = phi + pre * (jnp.exp(pre * pre * -0.5) * 0.3989422804014327)
        second = second + mm(act, down(fold))
    unit_two, rate_two = centre(second)
    live = live_ref[...]
    o_ref[...] = ((unit_two * gain_two + shift_two) * live).astype(BF16)
    grad_rows = cot_ref[...].astype(F32) * live
    grad_second = centre_back(grad_rows * gain_two, unit_two, rate_two).astype(BF16)
    gs_ref[...] = grad_second
    grad_normed = grad_second.astype(F32)
    grad_bias = []
    for fold in range(folds):
        cols = slice(fold * width, (fold + 1) * width)
        grad_hidden = (mm(gs_ref[...], down(fold), NT) * slope_ref[:, cols]).astype(BF16)
        gh_ref[:, cols] = grad_hidden
        grad_bias.append(column_sum(grad_hidden))
        grad_normed = grad_normed + mm(grad_hidden, up(fold), NT)
    grad_first = centre_back(grad_normed * gain_one, unit_one, rate_one).astype(BF16)
    gf_ref[...] = grad_first
    first = pl.program_id(0) == 0
    blank = jnp.zeros((2, width), F32)
    small = [
        column_sum(grad_first),
        column_sum(grad_normed * unit_one),
        column_sum(grad_normed),
        column_sum(grad_second),
        column_sum(grad_rows * unit_two),
        column_sum(grad_rows),
        blank,
    ]
    accumulate(small_ref, first, jnp.concatenate(small, axis=0))
    accumulate(gbias_ref, first, jnp.concatenate(grad_bias, axis=1))


def attend_back_kernel(rows, g_ref, w_ref, q_ref, k_ref, v_ref, p_ref, d_ref, gi_ref, small_ref):
    width = g_ref.shape[-1]
    grad_context = mm(g_ref[0], square(w_ref, 3 * rows, rows), NT).astype(BF16)
    for pair in range(HEADS // 2):
        cols = slice(pair * PAIR, (pair + 1) * PAIR)
        stacked = split_heads(grad_context[:, cols], 1.0)
        weights = p_ref[0, pair]
        grad_value = mm(weights.astype(BF16), stacked)
        grad_probs = mm(v_ref[0, :, cols], stacked, NT)
        inner = jnp.sum(weights * grad_probs, axis=0, keepdims=True)
        grad_scores = (weights * (grad_probs - inner)).astype(BF16)
        grad_key = mm(grad_scores, split_heads(q_ref[0, :, cols], HD**-0.5))
        grad_query = join_heads(mm(grad_scores, k_ref[0, :, cols], TN)) * HD**-0.5
        for part, grad in enumerate((grad_query, grad_key, grad_value)):
            at = part * width + pair * PAIR
            d_ref[0, :, at : at + PAIR] = grad.astype(BF16)
    total = g_ref[0].astype(F32)
    for part in range(3):
        grad = d_ref[0, :, part * width : (part + 1) * width]
        total = total + mm(grad, square(w_ref, part * rows, rows), NT)
    gi_ref[0] = total.astype(BF16)
    small = [
        column_sum(d_ref[0, :, :width]),
        column_sum(d_ref[0, :, 2 * width :]),
        jnp.zeros((6, width), F32),
    ]
    accumulate(small_ref, pl.program_id(0) == 0, jnp.concatenate(small, axis=0))


def whole(array):
    return pl.BlockSpec(
        array.shape, lambda i: (0,) * array.ndim, pipeline_mode=pl.Buffered(1)
    )


def kept(shape):
    return pl.BlockSpec(shape, lambda i: (0,) * len(shape))


def per_step(shape):
    return pl.BlockSpec((1,) + shape[1:], lambda i: (i,) + (0,) * (len(shape) - 1))


def shaped(shape, dtype):
    return jax.ShapeDtypeStruct(shape, dtype)


def attend(tokens, live, weights, rows, vec):
    seqs, slots, width = tokens.shape
    low = shaped((seqs, slots, width), BF16)
    outs = (
        low,
        low,
        low,
        shaped((seqs, HEADS // 2, slots, 2 * slots), F32),
        low,
        shaped((seqs, slots, width), F32),
    )
    return pl.pallas_call(
        partial(attend_kernel, rows),
        grid=(seqs,),
        in_specs=[per_step(tokens.shape), per_step(live.shape), whole(weights), whole(vec)],
        out_specs=tuple(per_step(out.shape) for out in outs),
        out_shape=outs,
        name="attend",
    )(tokens, live, weights, vec)


def feed(first_sum, live, cotangent, weights, rows, hidden, vec, bias):
    count, width = first_sum.shape
    block = 512 if count % 512 == 0 else 256
    inner = bias.shape[1]

    def tall(columns):
        return pl.BlockSpec((block, columns), lambda i: (i, 0))

    low = shaped((count, width), BF16)
    wide = shaped((count, inner), BF16)
    return pl.pallas_call(
        partial(feed_kernel, rows, hidden),
        grid=(count // block,),
        in_specs=[tall(width), tall(1), tall(width), whole(weights), whole(vec), whole(bias)],
        out_specs=(
            tall(width),
            tall(inner),
            tall(inner),
            tall(width),
            tall(width),
            tall(width),
            kept((8, width)),
            kept((1, inner)),
        ),
        out_shape=(low, wide, wide, low, low, low, shaped((8, width), F32), shaped((1, inner), F32)),
        scratch_shapes=[pltpu.VMEM((block, inner), F32)],
        name="feed",
    )(first_sum, live, cotangent, weights, vec, bias)


def attend_back(grad_first, weights, rows, query, key, value, probs):
    seqs, slots, width = grad_first.shape
    outs = (
        shaped((seqs, slots, 3 * width), BF16),
        shaped((seqs, slots, width), BF16),
        shaped((8, width), F32),
    )
    return pl.pallas_call(
        partial(attend_back_kernel, rows),
        grid=(seqs,),
        in_specs=[
            per_step(grad_first.shape),
            whole(weights),
            per_step(query.shape),
            per_step(query.shape),
            per_step(query.shape),
            per_step(probs.shape),
        ],
        out_specs=(per_step(outs[0].shape), per_step(outs[1].shape), kept((8, width))),
        out_shape=outs,
        name="attend_back",
    )(grad_first, weights, query, key, value, probs)


def scattered(packed):
    own = lax.psum_scatter(packed, "fsdp", scatter_dimension=0, tiled=True)[0]
    if lax.axis_size("rep") == 2:
        other = lax.ppermute(own, "rep", [(0, 1), (1, 0)])
        return own.astype(F32) + other.astype(F32)
    return lax.psum(own, "rep").astype(F32)


def unsharded(packed, sizes):
    pieces, at = [], 0
    for size in sizes:
        pieces.append(packed[:, at : at + size].reshape(-1, packed.shape[-1]))
        at += size
    return jnp.concatenate(pieces)[None]


def body(
    layer_input,
    slot_valid,
    projections,
    out_weight,
    vectors,
    up_weight,
    up_bias,
    down_weight,
    cotangent,
):
    seq_count, slot_count, width = layer_input.shape
    fsdp_size = lax.axis_size("fsdp")
    own_rows = out_weight.shape[0]
    hidden_own = down_weight.shape[0]
    folds = up_weight.shape[1] // width
    small = jnp.concatenate([vectors.reshape(-1), up_bias])
    small = jnp.pad(small, (0, SMALL_ROWS * width - small.size)).reshape(SMALL_ROWS, -1)
    attn_own = jnp.concatenate([projections.reshape(-1, width), out_weight, small])
    attn_all = lax.all_gather(attn_own, "fsdp", axis=0)
    ffn_own = jnp.concatenate(
        [up_weight[:, i * width : (i + 1) * width] for i in range(folds)] + [down_weight]
    )
    ffn_own = lax.optimization_barrier((ffn_own, attn_own))[0]
    ffn_all = lax.all_gather(ffn_own, "fsdp", axis=0)
    small_all = attn_all[:, 4 * own_rows :].reshape(fsdp_size, -1)
    vec_count = vectors.shape[0] * own_rows
    vec_all = (
        small_all[:, :vec_count]
        .reshape(fsdp_size, -1, own_rows)
        .transpose(1, 0, 2)
        .reshape(-1, width)
        .astype(F32)
    )
    bias_all = small_all[:, vec_count : vec_count + hidden_own].reshape(1, -1).astype(F32)
    attn_rows, ffn_rows, ffn_hidden = own_rows, own_rows, hidden_own
    if own_rows % 16:
        attn_all = unsharded(attn_all, [own_rows] * 4)
        ffn_all = unsharded(ffn_all, [own_rows] * folds + [hidden_own])
        attn_rows, ffn_rows, ffn_hidden = width, width, folds * width
    live = slot_valid.astype(F32)[:, :, None]
    query, key, value, probs, context, first_sum = attend(
        layer_input, live, attn_all, attn_rows, vec_all
    )
    token_count = seq_count * slot_count
    output, active, grad_hidden, grad_second, grad_first, normed, ffn_small, grad_bias = feed(
        first_sum.reshape(token_count, width),
        live.reshape(token_count, 1),
        cotangent.reshape(token_count, width),
        ffn_all,
        ffn_rows,
        ffn_hidden,
        vec_all,
        bias_all,
    )
    grad_down = jnp.dot(active.T, grad_second, preferred_element_type=F32).astype(BF16)
    grad_up = jnp.dot(normed.T, grad_hidden, preferred_element_type=F32).astype(BF16)
    up_blocks = grad_up.reshape(fsdp_size, own_rows, folds, width)
    ffn_parts = scattered(
        jnp.concatenate(
            [up_blocks[:, :, i] for i in range(folds)]
            + [grad_down.reshape(fsdp_size, hidden_own, width)],
            axis=1,
        )
    )
    grad_qkv, grad_input, attn_small = attend_back(
        grad_first.reshape(seq_count, slot_count, width), attn_all, attn_rows, query, key, value, probs
    )
    grad_out = jnp.dot(
        context.reshape(token_count, width).T, grad_first, preferred_element_type=F32
    )
    grad_stack = jnp.dot(
        layer_input.reshape(token_count, width).T,
        grad_qkv.reshape(token_count, 3 * width),
        preferred_element_type=F32,
    ).astype(BF16)
    grad_vectors = jnp.concatenate([attn_small[:2], ffn_small[:6]])
    small_grad = jnp.concatenate(
        [
            grad_vectors.reshape(-1, fsdp_size, own_rows).transpose(1, 0, 2).reshape(fsdp_size, -1),
            grad_bias.reshape(fsdp_size, -1),
        ],
        axis=1,
    ).astype(BF16)
    small_grad = jnp.pad(
        small_grad, ((0, 0), (0, SMALL_ROWS * width - small_grad.shape[1]))
    ).reshape(fsdp_size, SMALL_ROWS, width)
    attn_parts = scattered(
        jnp.concatenate(
            [
                grad_stack[:, i * width : (i + 1) * width].reshape(fsdp_size, own_rows, width)
                for i in range(3)
            ]
            + [grad_out.astype(BF16).reshape(fsdp_size, own_rows, width), small_grad],
            axis=1,
        )
    )
    small_part = attn_parts[4 * own_rows :].reshape(-1)
    return (
        output.reshape(layer_input.shape),
        grad_input,
        attn_parts[: 3 * own_rows].reshape(3, own_rows, width),
        attn_parts[3 * own_rows : 4 * own_rows],
        small_part[:vec_count].reshape(-1, own_rows),
        jnp.concatenate(
            [ffn_parts[i * own_rows : (i + 1) * own_rows] for i in range(folds)], axis=1
        ),
        small_part[vec_count : vec_count + hidden_own],
        ffn_parts[folds * own_rows :],
    )


def solution(mesh):
    rows3 = P(("fsdp", "rep"), None, None)
    third = P(None, "fsdp", None)
    tall = P("fsdp", None)
    return jax.shard_map(
        body,
        mesh=mesh,
        in_specs=(
            rows3,
            P(("fsdp", "rep"), None),
            third,
            tall,
            P(None, "fsdp"),
            tall,
            P("fsdp"),
            tall,
            rows3,
        ),
        out_specs=(rows3, rows3, third, tall, P(None, "fsdp"), tall, P("fsdp"), tall),
        check_vma=False,
    )
```

```python
from functools import partial

import jax
import jax.numpy as jnp
from jax import lax
from jax.experimental import pallas as pl
from jax.experimental.pallas import tpu as pltpu
from jax.sharding import PartitionSpec as P

HEADS = 12
HD = 64
PAIR = 2 * HD
SMALL_ROWS = 8
EPSILON = 1e-12
MASKED = -1e30
F32 = jnp.float32
BF16 = jnp.bfloat16
NN = (((1,), (0,)), ((), ()))
NT = (((1,), (1,)), ((), ()))
TN = (((0,), (0,)), ((), ()))


def mm(lhs, rhs, dims=NN):
    return lax.dot_general(lhs, rhs, dims, preferred_element_type=F32)


def square(ref, start, count):
    taken = ref[:, start : start + count, :]
    return taken.reshape(-1, taken.shape[-1])


def lane_masks(scale):
    lane = lax.broadcasted_iota(jnp.int32, (1, PAIR), 1)
    even = jnp.where(lane < HD, scale, 0.0).astype(BF16)
    odd = jnp.where(lane < HD, 0.0, scale).astype(BF16)
    return even, odd


def split_heads(pair, scale):
    even, odd = lane_masks(scale)
    return jnp.concatenate([pair * even, pair * odd], axis=0)


def join_heads(stacked):
    half = stacked.shape[0] // 2
    lane = lax.broadcasted_iota(jnp.int32, (half, PAIR), 1)
    return jnp.where(lane < HD, stacked[:half], stacked[half:])


def column_sum(values):
    return jnp.sum(values.astype(F32), axis=0, keepdims=True)


def attend_kernel(rows, x_ref, live_ref, w_ref, vec_ref, q_ref, k_ref, v_ref, p_ref, c_ref, f_ref):
    x = x_ref[0]
    q_ref[0] = (mm(x, square(w_ref, 0, rows)) + vec_ref[0:1]).astype(BF16)
    k_ref[0] = mm(x, square(w_ref, rows, rows)).astype(BF16)
    v_ref[0] = (mm(x, square(w_ref, 2 * rows, rows)) + vec_ref[1:2]).astype(BF16)
    live = live_ref[0] > 0.0
    for pair in range(HEADS // 2):
        cols = slice(pair * PAIR, (pair + 1) * PAIR)
        stacked = split_heads(q_ref[0, :, cols], HD**-0.5)
        scores = jnp.where(live, mm(k_ref[0, :, cols], stacked, NT), MASKED)
        raised = jnp.exp(scores - jnp.max(scores, axis=0, keepdims=True))
        weights = raised * (1.0 / jnp.sum(raised, axis=0, keepdims=True))
        p_ref[0, pair] = weights
        context = mm(weights.astype(BF16), v_ref[0, :, cols], TN)
        c_ref[0, :, cols] = join_heads(context).astype(BF16)
    f_ref[0] = x.astype(F32) + mm(c_ref[0], square(w_ref, 3 * rows, rows)) + vec_ref[2:3]


def centre(values):
    centered = values - jnp.mean(values, axis=-1, keepdims=True)
    spread = jnp.mean(centered * centered, axis=-1, keepdims=True)
    rate = lax.rsqrt(spread + EPSILON)
    return centered * rate, rate


def centre_back(grad, unit, rate):
    return rate * (
        grad
        - jnp.mean(grad, axis=-1, keepdims=True)
        - unit * jnp.mean(grad * unit, axis=-1, keepdims=True)
    )


def accumulate(ref, first, value):
    @pl.when(first)
    def _():
        ref[...] = value

    @pl.when(jnp.logical_not(first))
    def _():
        ref[...] += value


def feed_kernel(
    rows,
    hidden,
    f_ref,
    live_ref,
    cot_ref,
    w_ref,
    vec_ref,
    bias_ref,
    o_ref,
    act_ref,
    gh_ref,
    gs_ref,
    gf_ref,
    n_ref,
    small_ref,
    gbias_ref,
    slope_ref,
):
    width = f_ref.shape[-1]
    folds = act_ref.shape[-1] // width
    shards = max(width // hidden, 1)

    def up(fold):
        return square(w_ref, fold * rows, rows)

    def down(fold):
        base = folds * rows
        if hidden >= width:
            return square(w_ref, base + fold * width, width)
        taken = w_ref[fold * shards : (fold + 1) * shards, base : base + hidden, :]
        return taken.reshape(width, width)

    gain_one, shift_one, gain_two, shift_two = (vec_ref[i : i + 1] for i in (3, 4, 6, 7))
    unit_one, rate_one = centre(f_ref[...])
    normed = unit_one * gain_one + shift_one
    n_ref[...] = normed.astype(BF16)
    second = normed + vec_ref[5:6]
    for fold in range(folds):
        cols = slice(fold * width, (fold + 1) * width)
        pre = mm(n_ref[...], up(fold)) + bias_ref[:, cols]
        phi = 0.5 + 0.5 * lax.erf(pre * 0.7071067811865476)
        act = (pre * phi).astype(BF16)
        act_ref[:, cols] = act
        slope_ref[:, cols] = phi + pre * (jnp.exp(pre * pre * -0.5) * 0.3989422804014327)
        second = second + mm(act, down(fold))
    unit_two, rate_two = centre(second)
    live = live_ref[...]
    o_ref[...] = ((unit_two * gain_two + shift_two) * live).astype(BF16)
    grad_rows = cot_ref[...].astype(F32) * live
    grad_second = centre_back(grad_rows * gain_two, unit_two, rate_two).astype(BF16)
    gs_ref[...] = grad_second
    grad_normed = grad_second.astype(F32)
    grad_bias = []
    for fold in range(folds):
        cols = slice(fold * width, (fold + 1) * width)
        grad_hidden = (mm(gs_ref[...], down(fold), NT) * slope_ref[:, cols]).astype(BF16)
        gh_ref[:, cols] = grad_hidden
        grad_bias.append(column_sum(grad_hidden))
        grad_normed = grad_normed + mm(grad_hidden, up(fold), NT)
    grad_first = centre_back(grad_normed * gain_one, unit_one, rate_one).astype(BF16)
    gf_ref[...] = grad_first
    first = pl.program_id(0) == 0
    blank = jnp.zeros((2, width), F32)
    small = [
        column_sum(grad_first),
        column_sum(grad_normed * unit_one),
        column_sum(grad_normed),
        column_sum(grad_second),
        column_sum(grad_rows * unit_two),
        column_sum(grad_rows),
        blank,
    ]
    accumulate(small_ref, first, jnp.concatenate(small, axis=0))
    accumulate(gbias_ref, first, jnp.concatenate(grad_bias, axis=1))


def attend_back_kernel(rows, g_ref, w_ref, q_ref, k_ref, v_ref, p_ref, d_ref, gi_ref, small_ref):
    width = g_ref.shape[-1]
    grad_context = mm(g_ref[0], square(w_ref, 3 * rows, rows), NT).astype(BF16)
    for pair in range(HEADS // 2):
        cols = slice(pair * PAIR, (pair + 1) * PAIR)
        stacked = split_heads(grad_context[:, cols], 1.0)
        weights = p_ref[0, pair]
        grad_value = mm(weights.astype(BF16), stacked)
        grad_probs = mm(v_ref[0, :, cols], stacked, NT)
        inner = jnp.sum(weights * grad_probs, axis=0, keepdims=True)
        grad_scores = (weights * (grad_probs - inner)).astype(BF16)
        grad_key = mm(grad_scores, split_heads(q_ref[0, :, cols], HD**-0.5))
        grad_query = join_heads(mm(grad_scores, k_ref[0, :, cols], TN)) * HD**-0.5
        for part, grad in enumerate((grad_query, grad_key, grad_value)):
            at = part * width + pair * PAIR
            d_ref[0, :, at : at + PAIR] = grad.astype(BF16)
    total = g_ref[0].astype(F32)
    for part in range(3):
        grad = d_ref[0, :, part * width : (part + 1) * width]
        total = total + mm(grad, square(w_ref, part * rows, rows), NT)
    gi_ref[0] = total.astype(BF16)
    small = [
        column_sum(d_ref[0, :, :width]),
        column_sum(d_ref[0, :, 2 * width :]),
        jnp.zeros((6, width), F32),
    ]
    accumulate(small_ref, pl.program_id(0) == 0, jnp.concatenate(small, axis=0))


def whole(array):
    return pl.BlockSpec(
        array.shape, lambda i: (0,) * array.ndim, pipeline_mode=pl.Buffered(1)
    )


def kept(shape):
    return pl.BlockSpec(shape, lambda i: (0,) * len(shape))


def per_step(shape):
    return pl.BlockSpec((1,) + shape[1:], lambda i: (i,) + (0,) * (len(shape) - 1))


def shaped(shape, dtype):
    return jax.ShapeDtypeStruct(shape, dtype)


def attend(tokens, live, weights, rows, vec):
    seqs, slots, width = tokens.shape
    low = shaped((seqs, slots, width), BF16)
    outs = (
        low,
        low,
        low,
        shaped((seqs, HEADS // 2, slots, 2 * slots), F32),
        low,
        shaped((seqs, slots, width), F32),
    )
    return pl.pallas_call(
        partial(attend_kernel, rows),
        grid=(seqs,),
        in_specs=[per_step(tokens.shape), per_step(live.shape), whole(weights), whole(vec)],
        out_specs=tuple(per_step(out.shape) for out in outs),
        out_shape=outs,
        name="attend",
    )(tokens, live, weights, vec)


def feed(first_sum, live, cotangent, weights, rows, hidden, vec, bias):
    count, width = first_sum.shape
    block = 512 if count % 512 == 0 else 256
    inner = bias.shape[1]

    def tall(columns):
        return pl.BlockSpec((block, columns), lambda i: (i, 0))

    low = shaped((count, width), BF16)
    wide = shaped((count, inner), BF16)
    return pl.pallas_call(
        partial(feed_kernel, rows, hidden),
        grid=(count // block,),
        in_specs=[tall(width), tall(1), tall(width), whole(weights), whole(vec), whole(bias)],
        out_specs=(
            tall(width),
            tall(inner),
            tall(inner),
            tall(width),
            tall(width),
            tall(width),
            kept((8, width)),
            kept((1, inner)),
        ),
        out_shape=(low, wide, wide, low, low, low, shaped((8, width), F32), shaped((1, inner), F32)),
        scratch_shapes=[pltpu.VMEM((block, inner), F32)],
        name="feed",
    )(first_sum, live, cotangent, weights, vec, bias)


def attend_back(grad_first, weights, rows, query, key, value, probs):
    seqs, slots, width = grad_first.shape
    outs = (
        shaped((seqs, slots, 3 * width), BF16),
        shaped((seqs, slots, width), BF16),
        shaped((8, width), F32),
    )
    return pl.pallas_call(
        partial(attend_back_kernel, rows),
        grid=(seqs,),
        in_specs=[
            per_step(grad_first.shape),
            whole(weights),
            per_step(query.shape),
            per_step(query.shape),
            per_step(query.shape),
            per_step(probs.shape),
        ],
        out_specs=(per_step(outs[0].shape), per_step(outs[1].shape), kept((8, width))),
        out_shape=outs,
        name="attend_back",
    )(grad_first, weights, query, key, value, probs)


def slab_kernel(lhs_ref, rhs_ref, *refs):
    out_ref = refs[-1]
    out_ref[...] = mm(lhs_ref[...], rhs_ref[...], TN).reshape(out_ref.shape).astype(BF16)


def slab(lhs, rhs, packed, block, place, steps, lhs_moves):
    count, width = lhs.shape[0], packed.shape[-1]
    moving = pl.BlockSpec((count, width), lambda i: (0, i))
    still = pl.BlockSpec((count, width), lambda i: (0, 0))
    held = [] if isinstance(packed, jax.ShapeDtypeStruct) else [packed]
    return pl.pallas_call(
        slab_kernel,
        grid=(steps,),
        in_specs=[
            moving if lhs_moves else still,
            still if lhs_moves else moving,
        ]
        + [pl.BlockSpec(memory_space=pl.ANY)] * len(held),
        out_specs=pl.BlockSpec(block + (width,), place),
        out_shape=shaped(packed.shape, BF16),
        input_output_aliases={2: 0} if held else {},
        name="slab",
    )(lhs, rhs, *held)


def fan_kernel(rows, me_ref, x_ref, d_ref, small_ref, out_ref):
    step = pl.program_id(0)
    core, across, side = me_ref[0], me_ref[1], me_ref[2]
    width = x_ref.shape[-1]
    half = width // 2
    product = mm(x_ref[...], d_ref[...], TN)
    start = pl.multiple_of(step * rows, rows)
    for shard in range(width // rows):
        to_core, to_across, to_z = shard & 1, (shard >> 1) & 1, shard >> 2
        block = product[shard * rows : (shard + 1) * rows].astype(BF16)
        for to_side in range(2):
            cols = slice(to_side * half, (to_side + 1) * half)
            out_ref[
                to_core ^ core, to_side ^ side, to_across ^ across, to_z, pl.ds(start, rows), :
            ] = block[:, cols]

    @pl.when(step == 0)
    def _():
        for shard in range(width // rows):
            to_core, to_across, to_z = shard & 1, (shard >> 1) & 1, shard >> 2
            for to_side in range(2):
                cols = slice(to_side * half, (to_side + 1) * half)
                out_ref[
                    to_core ^ core,
                    to_side ^ side,
                    to_across ^ across,
                    to_z,
                    3 * rows : 3 * rows + SMALL_ROWS,
                    :,
                ] = small_ref[shard, :, cols]


def fan(tokens, grads, small, rows, me):
    count, width = tokens.shape
    shards = width // rows
    shape = (2, 2, 2, shards // 4, 3 * rows + SMALL_ROWS, width // 2)
    return pl.pallas_call(
        partial(fan_kernel, rows),
        grid=(3,),
        in_specs=[
            pl.BlockSpec(memory_space=pltpu.SMEM),
            pl.BlockSpec((count, width), lambda i: (0, 0)),
            pl.BlockSpec((count, width), lambda i: (0, i)),
            kept(small.shape),
        ],
        out_specs=kept(shape),
        out_shape=shaped(shape, BF16),
        name="fan",
    )(me, tokens, grads, small)


def plus(one, other):
    return (one.astype(F32) + other.astype(F32)).astype(BF16)


def stepwise(parts, z_now, side):
    size = lax.axis_size("fsdp")
    depth = size // 4
    swap_core = [(i, i ^ 1) for i in range(size)]
    swap_across = [(i, i ^ 2) for i in range(size)]
    swap_side = [(0, 1), (1, 0)]
    got = lax.ppermute(parts[1], "fsdp", swap_core)
    cut = parts.shape[-2] // 16 * 8
    one, two = slice(0, cut), slice(cut, None)

    def kept_part(side_at, across_at, rows):
        return plus(parts[0, side_at, across_at, :, rows], got[side_at, across_at, :, rows])

    side_sent = jnp.stack([kept_part(1, i, one) for i in range(2)])
    across_sent = jnp.stack([kept_part(i, 1, two) for i in range(2)])
    side_got = lax.ppermute(side_sent, "rep", swap_side)
    across_got = lax.ppermute(across_sent, "fsdp", swap_across)
    one_sent = plus(kept_part(0, 1, one), side_got[1])
    two_sent = plus(kept_part(1, 0, two), across_got[1])
    one_got = lax.ppermute(one_sent, "fsdp", swap_across)
    two_got = lax.ppermute(two_sent, "rep", swap_side)
    lines = jnp.concatenate(
        [
            plus(plus(kept_part(0, 0, one), side_got[0]), one_got),
            plus(plus(kept_part(0, 0, two), across_got[0]), two_got),
        ],
        axis=1,
    )
    total = lax.dynamic_index_in_dim(lines, z_now, 0, False).astype(F32)
    for hop in range(1, depth):
        sent = lax.dynamic_index_in_dim(lines, (z_now + hop) % depth, 0, False)
        turn = [(i, (i + 4 * hop) % size) for i in range(size)]
        total = total + lax.ppermute(sent, "fsdp", turn).astype(F32)
    own = total.astype(BF16)
    other = lax.ppermute(own, "rep", swap_side)
    low = jnp.where(side == 0, own, other)
    high = jnp.where(side == 0, other, own)
    return jnp.concatenate([low, high], axis=1).astype(F32)


def scattered(packed):
    own = lax.psum_scatter(packed, "fsdp", scatter_dimension=0, tiled=True)[0]
    if lax.axis_size("rep") == 2:
        other = lax.ppermute(own, "rep", [(0, 1), (1, 0)])
        return own.astype(F32) + other.astype(F32)
    return lax.psum(own, "rep").astype(F32)


def unsharded(packed, sizes):
    pieces, at = [], 0
    for size in sizes:
        pieces.append(packed[:, at : at + size].reshape(-1, packed.shape[-1]))
        at += size
    return jnp.concatenate(pieces)[None]


def body(
    layer_input,
    slot_valid,
    projections,
    out_weight,
    vectors,
    up_weight,
    up_bias,
    down_weight,
    cotangent,
):
    seq_count, slot_count, width = layer_input.shape
    fsdp_size = lax.axis_size("fsdp")
    own_rows = out_weight.shape[0]
    hidden_own = down_weight.shape[0]
    folds = up_weight.shape[1] // width
    small = jnp.concatenate([vectors.reshape(-1), up_bias])
    small = jnp.pad(small, (0, SMALL_ROWS * width - small.size)).reshape(SMALL_ROWS, -1)
    attn_own = jnp.concatenate([projections.reshape(-1, width), out_weight, small])
    attn_all = lax.all_gather(attn_own, "fsdp", axis=0)
    ffn_own = jnp.concatenate(
        [up_weight[:, i * width : (i + 1) * width] for i in range(folds)] + [down_weight]
    )
    ffn_own = lax.optimization_barrier((ffn_own, attn_own))[0]
    ffn_all = lax.all_gather(ffn_own, "fsdp", axis=0)
    small_all = attn_all[:, 4 * own_rows :].reshape(fsdp_size, -1)
    vec_count = vectors.shape[0] * own_rows
    vec_all = (
        small_all[:, :vec_count]
        .reshape(fsdp_size, -1, own_rows)
        .transpose(1, 0, 2)
        .reshape(-1, width)
        .astype(F32)
    )
    bias_all = small_all[:, vec_count : vec_count + hidden_own].reshape(1, -1).astype(F32)
    attn_rows, ffn_rows, ffn_hidden = own_rows, own_rows, hidden_own
    if own_rows % 16:
        attn_all = unsharded(attn_all, [own_rows] * 4)
        ffn_all = unsharded(ffn_all, [own_rows] * folds + [hidden_own])
        attn_rows, ffn_rows, ffn_hidden = width, width, folds * width
    live = slot_valid.astype(F32)[:, :, None]
    query, key, value, probs, context, first_sum = attend(
        layer_input, live, attn_all, attn_rows, vec_all
    )
    token_count = seq_count * slot_count
    output, active, grad_hidden, grad_second, grad_first, normed, ffn_small, grad_bias = feed(
        first_sum.reshape(token_count, width),
        live.reshape(token_count, 1),
        cotangent.reshape(token_count, width),
        ffn_all,
        ffn_rows,
        ffn_hidden,
        vec_all,
        bias_all,
    )
    tile = max(width // hidden_own, 1)
    packed_rows = folds * own_rows + hidden_own + own_rows
    packed = shaped((fsdp_size, packed_rows, width), BF16)
    packed = slab(
        active,
        grad_second,
        packed,
        (tile, hidden_own),
        lambda i: (i, folds * own_rows // hidden_own, 0),
        folds,
        True,
    )
    packed = slab(
        normed, grad_hidden, packed, (fsdp_size, own_rows), lambda i: (0, i, 0), folds, False
    )
    context = context.reshape(token_count, width)
    packed = slab(
        context,
        grad_first,
        packed,
        (fsdp_size, own_rows),
        lambda i: (0, packed_rows // own_rows - 1, 0),
        1,
        False,
    )
    ffn_parts = scattered(packed)
    grad_qkv, grad_input, attn_small = attend_back(
        grad_first.reshape(seq_count, slot_count, width), attn_all, attn_rows, query, key, value, probs
    )
    grad_vectors = jnp.concatenate([attn_small[:2], ffn_small[:6]])
    small_grad = jnp.concatenate(
        [
            grad_vectors.reshape(-1, fsdp_size, own_rows).transpose(1, 0, 2).reshape(fsdp_size, -1),
            grad_bias.reshape(fsdp_size, -1),
        ],
        axis=1,
    ).astype(BF16)
    small_grad = jnp.pad(
        small_grad, ((0, 0), (0, SMALL_ROWS * width - small_grad.shape[1]))
    ).reshape(fsdp_size, SMALL_ROWS, width)
    tokens = layer_input.reshape(token_count, width)
    grad_qkv = grad_qkv.reshape(token_count, 3 * width)
    if lax.axis_size("rep") == 2 and own_rows % 16 == 0:
        me = lax.axis_index("fsdp")
        side = lax.axis_index("rep")
        place = jnp.stack([me & 1, (me >> 1) & 1, side]).astype(jnp.int32)
        attn_parts = stepwise(fan(tokens, grad_qkv, small_grad, own_rows, place), me >> 2, side)
    else:
        packed = shaped((fsdp_size, 3 * own_rows, width), BF16)
        packed = slab(
            tokens, grad_qkv, packed, (fsdp_size, own_rows), lambda i: (0, i, 0), 3, False
        )
        attn_parts = scattered(jnp.concatenate([packed, small_grad], axis=1))
    small_part = attn_parts[3 * own_rows :].reshape(-1)
    return (
        output.reshape(layer_input.shape),
        grad_input,
        attn_parts[: 3 * own_rows].reshape(3, own_rows, width),
        ffn_parts[-own_rows:],
        small_part[:vec_count].reshape(-1, own_rows),
        jnp.concatenate(
            [ffn_parts[i * own_rows : (i + 1) * own_rows] for i in range(folds)], axis=1
        ),
        small_part[vec_count : vec_count + hidden_own],
        ffn_parts[folds * own_rows : folds * own_rows + hidden_own],
    )


def solution(mesh):
    rows3 = P(("fsdp", "rep"), None, None)
    third = P(None, "fsdp", None)
    tall = P("fsdp", None)
    return jax.shard_map(
        body,
        mesh=mesh,
        in_specs=(
            rows3,
            P(("fsdp", "rep"), None),
            third,
            tall,
            P(None, "fsdp"),
            tall,
            P("fsdp"),
            tall,
            rows3,
        ),
        out_specs=(rows3, rows3, third, tall, P(None, "fsdp"), tall, P("fsdp"), tall),
        check_vma=False,
    )
```
